512 devices in a mesh: vox: 32 (over y, z_hi, x), chan: 16 (over z_lo, core).
Axes of the slice: x: 4, y: 4, z: 16 (z_hi: 2, z_lo: 8; z = z_hi * 8 + z_lo), core: 2. Of those that a mesh axis runs over, the one named last changes fastest.
Arguments:
- activations: bfloat16 [1024, 32, 512], P('chan', 'vox'), may hold values from -6 to 6
- upstream: bfloat16 [512, 32, 512], P('chan', 'vox'), may hold values from -6 to 6
- weights: bfloat16 [512, 27, 1024], P('chan'), may hold values from -0.0390625 to 0.0390625
Outputs:
- outputs: bfloat16 [512, 32, 512], P('chan', 'vox')
- input_grad: bfloat16 [1024, 32, 512], P('chan', 'vox')
- weight_grad: bfloat16 [512, 27, 1024], P('chan')
The draws below stay inside these ranges and needn't reach their ends.
All inputs are finite; a program needn't handle non-finite values.
Results may differ from the reference program's by a relative error of at most 0.001.
Values may be sent and summed in bfloat16 or wider, within the bound.
No kernel may reach another device: no remote copies, remote signals or barrier semaphores. Data moves between devices by JAX's collectives and lax.ppermute only.
A program may use at most 128 MiB of HBM per device.

```python
import jax
import jax.numpy as jnp

CIN = 1024
COUT = 512
NY = 32
NZ = 16
NX = 32


def level_of(stream_key, shape, shards, least, high):
    def one(dim, blocks):
        heights = jax.random.uniform(jax.random.fold_in(jax.random.fold_in(stream_key, 6), dim), (blocks,), jnp.float32, least / len(shards), high / len(shards))
        return jnp.repeat(jnp.exp(heights), shape[dim] // blocks).reshape((-1,) + (1,) * (len(shape) - dim - 1))

    gain = one(*shards[0])
    for cut in shards[1:]:
        gain = gain * one(*cut)
    return gain


def scatter_about(own_key, extent, deviation, most, split=(), kind=jnp.bfloat16):
    values = jax.random.normal(own_key, extent, jnp.float32) * deviation
    if len(split) > 0:
        values = level_of(own_key, extent, split, -0.22, 0.18) * values
    return jnp.clip(values, min=-most, max=most).astype(kind)


def setup_inputs(seed: int = 0) -> dict:
    key_of = jax.random.split(jax.random.key(seed), 4)
    activations = scatter_about(key_of[0], (CIN, NX, NY * NZ), 1.0, 6.0, ((0, 16), (1, 32)))
    upstream = scatter_about(key_of[1], (COUT, NX, NY * NZ), 1.0, 6.0, ((0, 16), (1, 32)))
    weights = scatter_about(key_of[2], (COUT, 27, CIN), (27 * CIN) ** -0.5, 0.0390625, ((0, 16),))
    return dict(activations=activations, upstream=upstream, weights=weights)


tap_offsets = [(a, b, c) for a in (-1, 0, 1) for b in (-1, 0, 1) for c in (-1, 0, 1)]

def shifted(volume, off_x, off_y, off_z):
    channels = volume.shape[0]
    padded = jnp.pad(volume.reshape(channels, NX, NY, NZ), ((0, 0), (1, 1), (1, 1), (1, 1)))
    window = padded[:, 1 + off_x:1 + off_x + NX, 1 + off_y:1 + off_y + NY, 1 + off_z:1 + off_z + NZ]
    return window.reshape(channels, NX * NY * NZ)

def reference(activations, upstream, weights):
    up_flat = upstream.reshape(COUT, NX * NY * NZ)
    out_total = jnp.zeros((COUT, NX * NY * NZ), jnp.float32)
    grad_total = jnp.zeros((CIN, NX * NY * NZ), jnp.float32)
    weight_terms = []
    for index, offsets in enumerate(tap_offsets):
        moved = shifted(activations, offsets[0], offsets[1], offsets[2])
        back = shifted(upstream, -offsets[0], -offsets[1], -offsets[2])
        tap_weight = weights[:, index, :]
        out_total = out_total + jnp.dot(tap_weight, moved, preferred_element_type=jnp.float32)
        grad_total = grad_total + jnp.dot(tap_weight.T, back, preferred_element_type=jnp.float32)
        weight_terms.append(jnp.dot(up_flat, moved.T, preferred_element_type=jnp.float32))
    raw_grad = jnp.stack(weight_terms, axis=1)
    grad_scale = 1.0 / jnp.sqrt(jnp.float32(NX * NY * NZ))
    outputs = out_total.reshape(COUT, NX, NY * NZ).astype(jnp.bfloat16)
    input_grad = grad_total.reshape(CIN, NX, NY * NZ).astype(jnp.bfloat16)
    weight_grad = (raw_grad * grad_scale).astype(jnp.bfloat16)
    return (outputs, input_grad, weight_grad)
```

```python
import functools

import jax
import jax.numpy as jnp
from jax import lax
from jax.experimental import pallas as pl
from jax.experimental.pallas import tpu as pltpu
from jax.sharding import Mesh
from jax.sharding import PartitionSpec as P


NY = 32
NZ = 16
PLANE = NY * NZ
VOX = ("y", "zh", "x")
XY = ("y", "x")
CHAN = ("zl", "co")
F32 = jnp.float32
BF16 = jnp.bfloat16


def moved(value, b, c):
    step = NZ * b + c
    if step == 0:
        return value
    out = pltpu.roll(value, (-step) % PLANE, 1)
    lane = lax.broadcasted_iota(jnp.int32, value.shape, 1)
    keep = None
    if b != 0:
        keep = (lane + NZ * b >= 0) & (lane + NZ * b < PLANE)
    if c != 0:
        col = lane % NZ + c
        inside = (col >= 0) & (col < NZ)
        keep = inside if keep is None else keep & inside
    return jnp.where(keep, out, 0.0)


def forward_kernel(w_ref, x_ref, o_ref, x_rows):
    rows = o_ref.shape[1]
    cores, chips, ch = x_ref.shape[:3]
    for z in range(chips):
        for e in range(cores):
            first = (z * cores + e) * ch
            x_rows[first : first + ch, :] = x_ref[e, z]
    for a in range(3):
        y = jnp.dot(w_ref[9 * rows * a : 9 * rows * (a + 1), :], x_rows[...], preferred_element_type=F32)
        total = None
        for b in range(3):
            for c in range(3):
                k = 3 * b + c
                term = moved(y[rows * k : rows * (k + 1), :], b - 1, c - 1)
                total = term if total is None else total + term
        o_ref[a] = total


def forward(w_rows, x):
    rows = w_rows.shape[0] // 27
    return pl.pallas_call(
        forward_kernel,
        out_shape=jax.ShapeDtypeStruct((3, rows, PLANE), F32),
        scratch_shapes=[pltpu.VMEM((w_rows.shape[1], PLANE), BF16)],
        compiler_params=pltpu.CompilerParams(vmem_limit_bytes=32 * 2**20),
        name="forward_plane",
    )(w_rows, x)


def backward_kernel(w_ref, u_ref, o_ref, cols):
    rows = u_ref.shape[1]
    for a in range(3):
        plane = u_ref[2 - a].astype(F32)
        for b in range(3):
            for c in range(3):
                k = 9 * a + 3 * b + c
                cols[rows * k : rows * (k + 1), :] = moved(plane, 1 - b, 1 - c).astype(BF16)
    ch = o_ref.shape[2]
    cores = o_ref.shape[0]
    for z in range(o_ref.shape[1]):
        part = w_ref[:, ch * cores * z : ch * cores * (z + 1)]
        got = lax.dot_general(part, cols[...], (((0,), (0,)), ((), ())), preferred_element_type=F32)
        for e in range(cores):
            o_ref[e, z] = got[ch * e : ch * (e + 1)]


def backward(w_rows, planes, cores, chips):
    width = w_rows.shape[1]
    rows = planes.shape[1]
    return pl.pallas_call(
        backward_kernel,
        out_shape=jax.ShapeDtypeStruct((cores, chips, width // (cores * chips), PLANE), F32),
        scratch_shapes=[pltpu.VMEM((27 * rows, PLANE), BF16)],
        compiler_params=pltpu.CompilerParams(vmem_limit_bytes=32 * 2**20),
        name="backward_plane",
    )(w_rows, planes)


def filter_kernel(a_ref, u_ref, o_ref, lhs, rhs, acc):
    run, chans = a_ref.shape[0], a_ref.shape[1]
    rows = u_ref.shape[2]

    @pl.when(pl.program_id(0) == 0)
    def _():
        acc[...] = jnp.zeros_like(acc)

    for q in range(run + 2):
        if q == 0:
            plane = u_ref[0, 1]
        elif q == run + 1:
            plane = u_ref[run - 1, 1]
        else:
            plane = u_ref[q - 1, 0]
        plane = plane.astype(F32)
        for c in range(3):
            lhs[q, rows * c : rows * (c + 1), :] = moved(plane, 0, 1 - c).astype(BF16)
    for q in range(run):
        plane = a_ref[q].astype(F32)
        for b in range(3):
            rhs[q, chans * b : chans * (b + 1), :] = moved(plane, b - 1, 0).astype(BF16)
    total = acc[...]
    for q in range(run):
        left = lhs[q : q + 3].reshape(9 * rows, PLANE)
        total = total + lax.dot_general(left, rhs[q], (((1,), (1,)), ((), ())), preferred_element_type=F32)
    acc[...] = total

    @pl.when(pl.program_id(0) == pl.num_programs(0) - 1)
    def _():
        low = lax.broadcasted_iota(jnp.int32, (8, 128), 1) < 64
        for k in range(27):
            a, b, c = k // 9, k // 3 % 3, k % 3
            for h in range(o_ref.shape[0]):
                row = rows * (3 * (2 - a) + c) + 16 * h
                if b == 2:
                    one = total[row : row + 8, 128:192]
                    two = total[row + 8 : row + 16, 128:192]
                    o_ref[h, k] = jnp.concatenate([one, two], axis=1)
                else:
                    one = total[row : row + 8, 0:128]
                    two = total[row + 8 : row + 16, 0:128]
                    if b == 0:
                        two = pltpu.roll(two, 64, 1)
                    else:
                        one = pltpu.roll(one, 64, 1)
                    o_ref[h, k] = jnp.where(low, one, two)


def filter_grad(acts, ups, runs):
    planes, chans = acts.shape[0], acts.shape[1]
    rows = ups.shape[2]
    run = planes // runs
    return pl.pallas_call(
        filter_kernel,
        grid=(runs,),
        in_specs=[
            pl.BlockSpec((run, chans, PLANE), lambda r: (r, 0, 0)),
            pl.BlockSpec((run, 2, rows, PLANE), lambda r: (r, 0, 0, 0)),
        ],
        out_specs=pl.BlockSpec((rows // 16, 27, 8, 128), lambda r: (0, 0, 0, 0)),
        out_shape=jax.ShapeDtypeStruct((rows // 16, 27, 8, 128), F32),
        scratch_shapes=[
            pltpu.VMEM((run + 2, 3 * rows, PLANE), BF16),
            pltpu.VMEM((run, 3 * chans, PLANE), BF16),
            pltpu.VMEM((9 * rows, 3 * chans), F32),
        ],
        compiler_params=pltpu.CompilerParams(vmem_limit_bytes=32 * 2**20),
        name="filter_planes",
    )(acts, ups)


def join_kernel(r_ref, o_ref, *, order):
    low = lax.broadcasted_iota(jnp.int32, (8, 128), 1) < 64
    for k in range(o_ref.shape[0]):
        for t in range(len(order) // 2):
            for h in range(r_ref.shape[1]):
                left = r_ref[order[2 * t], h, k].astype(F32)
                right = r_ref[order[2 * t + 1], h, k].astype(F32)
                one = jnp.where(low, left, pltpu.roll(right, 64, 1))
                two = jnp.where(low, pltpu.roll(left, 64, 1), right)
                both = jnp.concatenate([one, two], axis=0).astype(BF16)
                o_ref[k, 16 * h : 16 * (h + 1), 128 * t : 128 * (t + 1)] = both


def join(pieces, order):
    size, halves = pieces.shape[:2]
    return pl.pallas_call(
        functools.partial(join_kernel, order=order),
        grid=(9,),
        in_specs=[pl.BlockSpec((size, halves, 3, 8, 128), lambda g: (0, 0, g, 0, 0))],
        out_specs=pl.BlockSpec((3, 16 * halves, 64 * size), lambda g: (g, 0, 0)),
        out_shape=jax.ShapeDtypeStruct((27, 16 * halves, 64 * size), BF16),
        name="join_pieces",
    )(pieces)


def exchange(pieces, axes):
    return lax.all_to_all(pieces, axes, 0, 0, tiled=True)


def shared(value, axes):
    return exchange(jnp.broadcast_to(value, (lax.axis_size(axes), *value.shape)), axes)


def local(activations, upstream, weights):
    ch, co = activations.shape[0], upstream.shape[0]
    n_vox, n_x, n_y = lax.axis_size(VOX), lax.axis_size("x"), lax.axis_size("y")
    n_zl, n_co = lax.axis_size("zl"), lax.axis_size("co")
    n_xy = n_x * n_y
    cin = ch * n_zl * n_co
    up = [(i, i + 1) for i in range(n_vox - 1)]
    down = [(i + 1, i) for i in range(n_vox - 1)]
    act = activations.reshape(ch, PLANE)
    ups = upstream.reshape(co, PLANE)

    near = shared(act, "zl")

    before = lax.ppermute(ups, VOX, up)
    after = lax.ppermute(ups, VOX, down)
    edge = jnp.where(lax.axis_index("x") == 0, before, after)
    up_planes = jnp.stack([ups, edge])
    up_planes = lax.all_gather(up_planes, XY, axis=0, tiled=False)

    w_rows = weights.transpose(1, 0, 2).reshape(27 * co, cin)
    part = backward(w_rows, jnp.stack([before, ups, after]), n_co, n_zl)
    part = exchange(part, "co")
    part = jnp.sum(part, axis=0)
    part = lax.psum_scatter(part.reshape(n_zl * ch, PLANE), "zl", scatter_dimension=0, tiled=True)
    input_grad = part.astype(BF16).reshape(ch, 1, PLANE)

    plane = shared(near, "co")

    acts = exchange(plane.reshape(n_xy, ch, PLANE), XY)
    around = forward(w_rows, plane)
    from_after = lax.ppermute(around[2], VOX, down)
    from_before = lax.ppermute(around[0], VOX, up)
    outputs = (around[1] + from_after + from_before).astype(BF16).reshape(co, 1, PLANE)

    raw = filter_grad(acts, up_planes, n_y)
    raw = exchange(raw, "zh")
    raw = jnp.sum(raw, axis=0)
    scale = 1.0 / jnp.sqrt(jnp.float32(n_vox * PLANE))
    mine = (raw * scale).astype(BF16)
    halves = shared(mine, "zh")
    pieces = shared(halves, XY)
    order = tuple(e * n_zl + z for z in range(n_zl) for e in range(n_co))
    weight_grad = join(pieces, order).transpose(1, 0, 2)
    return (outputs, input_grad, weight_grad)


def solution(mesh):
    finer = Mesh(mesh.devices.reshape(SPLIT), ("y", "zh", "x", "zl", "co"))
    specs = (P(CHAN, VOX, None), P(CHAN, VOX, None), P(CHAN, None, None))

    return jax.shard_map(local, mesh=finer, in_specs=specs, out_specs=specs, check_vma=False)


SPLIT = (4, 2, 4, 8, 2)
```

```python
import functools

import jax
import jax.numpy as jnp
from jax import lax
from jax.experimental import pallas as pl
from jax.experimental.pallas import tpu as pltpu
from jax.sharding import Mesh
from jax.sharding import PartitionSpec as P


NY = 32
NZ = 16
PLANE = NY * NZ
VOX = ("y", "zh", "x")
XY = ("y", "x")
CHAN = ("zl", "co")
F32 = jnp.float32
BF16 = jnp.bfloat16


def moved(value, b, c):
    step = NZ * b + c
    if step == 0:
        return value
    out = pltpu.roll(value, (-step) % PLANE, 1)
    lane = lax.broadcasted_iota(jnp.int32, value.shape, 1)
    keep = None
    if b != 0:
        keep = (lane + NZ * b >= 0) & (lane + NZ * b < PLANE)
    if c != 0:
        col = lane % NZ + c
        inside = (col >= 0) & (col < NZ)
        keep = inside if keep is None else keep & inside
    return jnp.where(keep, out, 0.0)


def forward_kernel(w_ref, x_ref, o_ref, x_rows):
    rows = o_ref.shape[1]
    cores, chips, ch = x_ref.shape[:3]
    for z in range(chips):
        for e in range(cores):
            first = (z * cores + e) * ch
            x_rows[first : first + ch, :] = x_ref[e, z]
    for a in range(3):
        y = jnp.dot(w_ref[9 * rows * a : 9 * rows * (a + 1), :], x_rows[...], preferred_element_type=F32)
        total = None
        for b in range(3):
            for c in range(3):
                k = 3 * b + c
                term = moved(y[rows * k : rows * (k + 1), :], b - 1, c - 1)
                total = term if total is None else total + term
        o_ref[a] = total


def forward(w_rows, x):
    rows = w_rows.shape[0] // 27
    return pl.pallas_call(
        forward_kernel,
        out_shape=jax.ShapeDtypeStruct((3, rows, PLANE), F32),
        scratch_shapes=[pltpu.VMEM((w_rows.shape[1], PLANE), BF16)],
        compiler_params=pltpu.CompilerParams(vmem_limit_bytes=32 * 2**20),
        name="forward_plane",
    )(w_rows, x)


def backward_kernel(w_ref, u_ref, o_ref, cols):
    rows = u_ref.shape[1]
    for a in range(3):
        plane = u_ref[2 - a].astype(F32)
        for b in range(3):
            for c in range(3):
                k = 9 * a + 3 * b + c
                cols[rows * k : rows * (k + 1), :] = moved(plane, 1 - b, 1 - c).astype(BF16)
    ch = o_ref.shape[1]
    for t in range(o_ref.shape[0]):
        part = w_ref[:, ch * t : ch * (t + 1)]
        o_ref[t] = lax.dot_general(part, cols[...], (((0,), (0,)), ((), ())), preferred_element_type=F32)


def backward(w_rows, planes):
    width = w_rows.shape[1]
    rows = planes.shape[1]
    return pl.pallas_call(
        backward_kernel,
        out_shape=jax.ShapeDtypeStruct((width // 128, 128, PLANE), F32),
        scratch_shapes=[pltpu.VMEM((27 * rows, PLANE), BF16)],
        compiler_params=pltpu.CompilerParams(vmem_limit_bytes=32 * 2**20),
        name="backward_plane",
    )(w_rows, planes)


def filter_kernel(own_ref, a_ref, u_ref, o_ref, lhs, rhs, acc):
    run, chans = a_ref.shape[0], a_ref.shape[1]
    rows = u_ref.shape[3]

    @pl.when(pl.program_id(0) == 0)
    def _():
        acc[...] = jnp.zeros_like(acc)

    for q in range(run + 2):
        holder = min(max(q - 1, 0), run - 1)
        entry = lax.rem(own_ref[1] - holder + run, run)
        plane = u_ref[0, entry, 0 if holder == q - 1 else 1].astype(F32)
        for c in range(3):
            lhs[q, rows * c : rows * (c + 1), :] = moved(plane, 0, 1 - c).astype(BF16)
    for q in range(run):
        plane = a_ref[q].astype(F32)
        for b in range(3):
            rhs[q, chans * b : chans * (b + 1), :] = moved(plane, b - 1, 0).astype(BF16)
    total = acc[...]
    for q in range(run):
        left = lhs[q : q + 3].reshape(9 * rows, PLANE)
        total = total + lax.dot_general(left, rhs[q], (((1,), (1,)), ((), ())), preferred_element_type=F32)
    acc[...] = total

    @pl.when(pl.program_id(0) == pl.num_programs(0) - 1)
    def _():
        low = lax.broadcasted_iota(jnp.int32, (8, 128), 1) < 64
        for k in range(27):
            a, b, c = k // 9, k // 3 % 3, k % 3
            for h in range(o_ref.shape[0]):
                row = rows * (3 * (2 - a) + c) + 16 * h
                if b == 2:
                    one = total[row : row + 8, 128:192]
                    two = total[row + 8 : row + 16, 128:192]
                    o_ref[h, k] = jnp.concatenate([one, two], axis=1)
                else:
                    one = total[row : row + 8, 0:128]
                    two = total[row + 8 : row + 16, 0:128]
                    if b == 0:
                        two = pltpu.roll(two, 64, 1)
                    else:
                        one = pltpu.roll(one, 64, 1)
                    o_ref[h, k] = jnp.where(low, one, two)


def filter_grad(acts, ups, own):
    chans = acts.shape[1]
    runs, run, _, rows = ups.shape[:4]
    spec = pltpu.PrefetchScalarGridSpec(
        num_scalar_prefetch=1,
        grid=(runs,),
        in_specs=[
            pl.BlockSpec((run, chans, PLANE), lambda r, own: (r, 0, 0)),
            pl.BlockSpec((1, run, 2, rows, PLANE), lambda r, own: (lax.rem(own[0] - r + runs, runs), 0, 0, 0, 0)),
        ],
        out_specs=pl.BlockSpec((rows // 16, 27, 8, 128), lambda r, own: (0, 0, 0, 0)),
        scratch_shapes=[
            pltpu.VMEM((run + 2, 3 * rows, PLANE), BF16),
            pltpu.VMEM((run, 3 * chans, PLANE), BF16),
            pltpu.VMEM((9 * rows, 3 * chans), F32),
        ],
    )
    return pl.pallas_call(
        filter_kernel,
        grid_spec=spec,
        out_shape=jax.ShapeDtypeStruct((rows // 16, 27, 8, 128), F32),
        compiler_params=pltpu.CompilerParams(vmem_limit_bytes=32 * 2**20),
        name="filter_planes",
    )(own, acts, ups)


def join_kernel(r_ref, o_ref, *, order):
    low = lax.broadcasted_iota(jnp.int32, (8, 128), 1) < 64
    for k in range(o_ref.shape[0]):
        for t in range(len(order) // 2):
            for h in range(r_ref.shape[1]):
                left = r_ref[order[2 * t], h, k].astype(F32)
                right = r_ref[order[2 * t + 1], h, k].astype(F32)
                one = jnp.where(low, left, pltpu.roll(right, 64, 1))
                two = jnp.where(low, pltpu.roll(left, 64, 1), right)
                both = jnp.concatenate([one, two], axis=0).astype(BF16)
                o_ref[k, 16 * h : 16 * (h + 1), 128 * t : 128 * (t + 1)] = both


def join(pieces, order):
    size, halves = pieces.shape[:2]
    return pl.pallas_call(
        functools.partial(join_kernel, order=order),
        grid=(9,),
        in_specs=[pl.BlockSpec((size, halves, 3, 8, 128), lambda g: (0, 0, g, 0, 0))],
        out_specs=pl.BlockSpec((3, 16 * halves, 64 * size), lambda g: (g, 0, 0)),
        out_shape=jax.ShapeDtypeStruct((27, 16 * halves, 64 * size), BF16),
        name="join_pieces",
    )(pieces)


def exchange(pieces, axes):
    return lax.all_to_all(pieces, axes, 0, 0, tiled=True)


def shared(value, axes):
    return exchange(jnp.broadcast_to(value, (lax.axis_size(axes), *value.shape)), axes)


def from_before(value, axis):
    size = lax.axis_size(axis)
    pieces = [value]
    for d in range(1, size):
        pieces.append(lax.ppermute(value, axis, [(i, (i + d) % size) for i in range(size)]))
    return pieces


def local(activations, upstream, weights):
    ch, co = activations.shape[0], upstream.shape[0]
    n_vox, n_x, n_y = lax.axis_size(VOX), lax.axis_size("x"), lax.axis_size("y")
    n_zl, n_co = lax.axis_size("zl"), lax.axis_size("co")
    n_xy = n_x * n_y
    cin = ch * n_zl * n_co
    up = [(i, i + 1) for i in range(n_vox - 1)]
    down = [(i + 1, i) for i in range(n_vox - 1)]
    act = activations.reshape(ch, PLANE)
    ups = upstream.reshape(co, PLANE)

    near = shared(act, "zl")

    before = lax.ppermute(ups, VOX, up)
    after = lax.ppermute(ups, VOX, down)
    edge = jnp.where(lax.axis_index("x") == 0, before, after)
    up_planes = jnp.stack([ups, edge])
    row = jnp.stack(from_before(up_planes, "x"))
    up_planes = jnp.stack(from_before(row, "y"))

    w_rows = weights.transpose(1, 0, 2).reshape(27 * co, cin)
    part = backward(w_rows, jnp.stack([before, ups, after]))
    part = lax.psum_scatter(part.reshape(cin, PLANE), CHAN, scatter_dimension=0, tiled=True)
    input_grad = part.astype(BF16).reshape(ch, 1, PLANE)

    plane = shared(near, "co")

    acts = exchange(plane.reshape(n_xy, ch, PLANE), XY)
    around = forward(w_rows, plane)
    after_part = lax.ppermute(around[2], VOX, down)
    before_part = lax.ppermute(around[0], VOX, up)
    outputs = (around[1] + after_part + before_part).astype(BF16).reshape(co, 1, PLANE)

    raw = filter_grad(acts, up_planes, jnp.stack([lax.axis_index("y"), lax.axis_index("x")]))
    raw = exchange(raw, "zh")
    raw = jnp.sum(raw, axis=0)
    scale = 1.0 / jnp.sqrt(jnp.float32(n_vox * PLANE))
    mine = (raw * scale).astype(BF16)
    halves = shared(mine, "zh")
    pieces = shared(halves, XY)
    order = tuple(e * n_zl + z for z in range(n_zl) for e in range(n_co))
    weight_grad = join(pieces, order).transpose(1, 0, 2)
    return (outputs, input_grad, weight_grad)


def solution(mesh):
    finer = Mesh(mesh.devices.reshape(SPLIT), ("y", "zh", "x", "zl", "co"))
    specs = (P(CHAN, VOX, None), P(CHAN, VOX, None), P(CHAN, None, None))

    return jax.shard_map(local, mesh=finer, in_specs=specs, out_specs=specs, check_vma=False)


SPLIT = (4, 2, 4, 8, 2)
```

```python
import jax
import jax.numpy as jnp
from jax import lax
from jax.experimental import pallas as pl
from jax.experimental.pallas import tpu as pltpu
from jax.sharding import Mesh
from jax.sharding import PartitionSpec as P


NY = 32
NZ = 16
PLANE = NY * NZ
VOX = ("y", "zh", "x")
XY = ("y", "x")
CHAN = ("zl", "co")
F32 = jnp.float32
BF16 = jnp.bfloat16


def moved(value, b, c):
    step = NZ * b + c
    if step == 0:
        return value
    out = pltpu.roll(value, (-step) % PLANE, 1)
    lane = lax.broadcasted_iota(jnp.int32, value.shape, 1)
    keep = None
    if b != 0:
        keep = (lane + NZ * b >= 0) & (lane + NZ * b < PLANE)
    if c != 0:
        col = lane % NZ + c
        inside = (col >= 0) & (col < NZ)
        keep = inside if keep is None else keep & inside
    return jnp.where(keep, out, 0.0)


def forward_kernel(w_ref, low_ref, high_ref, o_ref, x_rows):
    rows = o_ref.shape[1]
    cores, chips, ch = low_ref.shape[:3]
    for z in range(chips):
        for e in range(cores):
            for half, ref in enumerate((low_ref, high_ref)):
                first = ((z * cores + e) * 2 + half) * ch
                x_rows[first : first + ch, :] = ref[e, z]
    for a in range(3):
        y = jnp.dot(w_ref[9 * rows * a : 9 * rows * (a + 1), :], x_rows[...], preferred_element_type=F32)
        total = None
        for b in range(3):
            for c in range(3):
                k = 3 * b + c
                term = moved(y[rows * k : rows * (k + 1), :], b - 1, c - 1)
                total = term if total is None else total + term
        o_ref[a] = total


def forward(w_rows, low, high):
    rows = w_rows.shape[0] // 27
    return pl.pallas_call(
        forward_kernel,
        out_shape=jax.ShapeDtypeStruct((3, rows, PLANE), F32),
        scratch_shapes=[pltpu.VMEM((w_rows.shape[1], PLANE), BF16)],
        compiler_params=pltpu.CompilerParams(vmem_limit_bytes=32 * 2**20),
        name="forward_plane",
    )(w_rows, low, high)


def backward_kernel(w_ref, u_ref, o_ref, cols):
    rows = u_ref.shape[1]
    for a in range(3):
        plane = u_ref[2 - a].astype(F32)
        for b in range(3):
            for c in range(3):
                k = 9 * a + 3 * b + c
                cols[rows * k : rows * (k + 1), :] = moved(plane, 1 - b, 1 - c).astype(BF16)
    ch = o_ref.shape[1]
    for t in range(o_ref.shape[0]):
        part = w_ref[:, ch * t : ch * (t + 1)]
        o_ref[t] = lax.dot_general(part, cols[...], (((0,), (0,)), ((), ())), preferred_element_type=F32)


def backward(w_rows, planes):
    width = w_rows.shape[1]
    rows = planes.shape[1]
    return pl.pallas_call(
        backward_kernel,
        out_shape=jax.ShapeDtypeStruct((width // 128, 128, PLANE), F32),
        scratch_shapes=[pltpu.VMEM((27 * rows, PLANE), BF16)],
        compiler_params=pltpu.CompilerParams(vmem_limit_bytes=32 * 2**20),
        name="backward_plane",
    )(w_rows, planes)


def filter_kernel(a_ref, u_ref, o_ref, lhs, rhs, acc):
    cores, run, chans = a_ref.shape[:3]
    rows = (u_ref.shape[1] - chans) // 2

    @pl.when(pl.program_id(0) == 0)
    def _():
        acc[...] = jnp.zeros_like(acc)

    for q in range(run + 2):
        holder = min(max(q - 1, 0), run - 1)
        first = chans if holder == q - 1 else chans + rows
        plane = u_ref[holder, first : first + rows, :].astype(F32)
        for c in range(3):
            lhs[q, rows * c : rows * (c + 1), :] = moved(plane, 0, 1 - c).astype(BF16)
    for q in range(run):
        for e in range(cores):
            plane = a_ref[e, q].astype(F32)
            for b in range(3):
                first = chans * (cores * b + e)
                rhs[q, first : first + chans, :] = moved(plane, b - 1, 0).astype(BF16)
    total = acc[...]
    for q in range(run):
        left = lhs[q : q + 3].reshape(9 * rows, PLANE)
        total = total + lax.dot_general(left, rhs[q], (((1,), (1,)), ((), ())), preferred_element_type=F32)
    acc[...] = total

    @pl.when(pl.program_id(0) == pl.num_programs(0) - 1)
    def _():
        group = lax.broadcasted_iota(jnp.int32, (8, 128), 1) // 32
        for k in range(27):
            a, b, c = k // 9, k // 3 % 3, k % 3
            for h in range(o_ref.shape[0]):
                row = rows * (3 * (2 - a) + c) + 16 * h
                sides = []
                for first in (row, row + 8):
                    if b == 2:
                        side = total[first : first + 8, 128:192]
                        side = jnp.concatenate([side, side], axis=1)
                    else:
                        side = total[first : first + 8, 0:128]
                    sides.append(pltpu.roll(side, 64, 1) if b == 1 else side)
                one, two = sides
                left = jnp.where(group == 0, one, pltpu.roll(two, 32, 1))
                right = jnp.where(group == 2, pltpu.roll(one, 32, 1), pltpu.roll(two, 64, 1))
                o_ref[h, k] = jnp.where(group < 2, left, right)


def filter_grad(acts, mixed, runs):
    cores, planes, chans = acts.shape[:3]
    height = mixed.shape[1]
    rows = (height - chans) // 2
    run = planes // runs
    return pl.pallas_call(
        filter_kernel,
        grid=(runs,),
        in_specs=[
            pl.BlockSpec((cores, run, chans, PLANE), lambda r: (0, r, 0, 0)),
            pl.BlockSpec((run, height, PLANE), lambda r: (r, 0, 0)),
        ],
        out_specs=pl.BlockSpec((rows // 16, 27, 8, 128), lambda r: (0, 0, 0, 0)),
        out_shape=jax.ShapeDtypeStruct((rows // 16, 27, 8, 128), F32),
        scratch_shapes=[
            pltpu.VMEM((run + 2, 3 * rows, PLANE), BF16),
            pltpu.VMEM((run, 3 * cores * chans, PLANE), BF16),
            pltpu.VMEM((9 * rows, 3 * cores * chans), F32),
        ],
        compiler_params=pltpu.CompilerParams(vmem_limit_bytes=32 * 2**20),
        name="filter_planes",
    )(acts, mixed)


def join_kernel(r_ref, o_ref):
    even = lax.broadcasted_iota(jnp.int32, (8, 128), 1) // 32 % 2 == 0
    for k in range(o_ref.shape[0]):
        for t in range(r_ref.shape[0] // 2):
            for h in range(r_ref.shape[1]):
                left = r_ref[2 * t, h, k].astype(F32)
                right = r_ref[2 * t + 1, h, k].astype(F32)
                one = jnp.where(even, left, pltpu.roll(right, 32, 1))
                two = jnp.where(even, pltpu.roll(left, 96, 1), right)
                both = jnp.concatenate([one, two], axis=0).astype(BF16)
                o_ref[k, 16 * h : 16 * (h + 1), 128 * t : 128 * (t + 1)] = both


def join(pieces):
    size, halves = pieces.shape[:2]
    return pl.pallas_call(
        join_kernel,
        grid=(9,),
        in_specs=[pl.BlockSpec((size, halves, 3, 8, 128), lambda g: (0, 0, g, 0, 0))],
        out_specs=pl.BlockSpec((3, 16 * halves, 64 * size), lambda g: (g, 0, 0)),
        out_shape=jax.ShapeDtypeStruct((27, 16 * halves, 64 * size), BF16),
        name="join_pieces",
    )(pieces)


def exchange(pieces, axes):
    return lax.all_to_all(pieces, axes, 0, 0, tiled=True)


def shared(value, axes):
    return exchange(jnp.broadcast_to(value, (lax.axis_size(axes), *value.shape)), axes)


def local(activations, upstream, weights):
    ch, co = activations.shape[0], upstream.shape[0]
    n_vox, n_y = lax.axis_size(VOX), lax.axis_size("y")
    n_xy, n_chan = lax.axis_size(XY), lax.axis_size(CHAN)
    cin = ch * n_chan
    up = [(i, i + 1) for i in range(n_vox - 1)]
    down = [(i + 1, i) for i in range(n_vox - 1)]
    act = activations.reshape(ch, PLANE)
    ups = upstream.reshape(co, PLANE)

    before = lax.ppermute(ups, VOX, up)
    after = lax.ppermute(ups, VOX, down)

    near = shared(act, "zl")

    w_rows = weights.transpose(1, 0, 2).reshape(27 * co, cin)
    part = backward(w_rows, jnp.stack([before, ups, after]))
    part = lax.psum_scatter(part.reshape(cin, PLANE), CHAN, scatter_dimension=0, tiled=True)
    input_grad = part.astype(BF16).reshape(ch, 1, PLANE)

    edge = jnp.where(lax.axis_index("x") == 0, before, after)
    planes = jnp.broadcast_to(jnp.concatenate([ups, edge]), (n_xy, 2 * co, PLANE))
    mixed = jnp.concatenate([near.reshape(n_xy, cin // (2 * n_xy), PLANE), planes], axis=1)
    mixed = exchange(mixed, XY)

    low = lax.all_gather(near[:, : ch // 2], "co", axis=0, tiled=False)
    high = lax.all_gather(near[:, ch // 2 :], "co", axis=0, tiled=False)
    around = forward(w_rows, low, high)
    after_part = lax.ppermute(around[2], VOX, down)
    before_part = lax.ppermute(around[0], VOX, up)
    outputs = (around[1] + after_part + before_part).astype(BF16).reshape(co, 1, PLANE)

    acts = shared(mixed[:, : cin // (2 * n_xy)], "co")
    raw = filter_grad(acts, mixed, n_y)
    raw = exchange(raw, "zh")
    raw = jnp.sum(raw, axis=0)
    scale = 1.0 / jnp.sqrt(jnp.float32(n_vox * PLANE))
    mine = (raw * scale).astype(BF16)
    halves = shared(mine, "zh")
    pieces = shared(halves, XY)
    weight_grad = join(pieces).transpose(1, 0, 2)
    return (outputs, input_grad, weight_grad)


def solution(mesh):
    finer = Mesh(mesh.devices.reshape(SPLIT), ("y", "zh", "x", "zl", "co"))
    specs = (P(CHAN, VOX, None), P(CHAN, VOX, None), P(CHAN, None, None))

    return jax.shard_map(local, mesh=finer, in_specs=specs, out_specs=specs, check_vma=False)


SPLIT = (4, 2, 4, 8, 2)
```

```python
import jax
import jax.numpy as jnp
from jax import lax
from jax.experimental import pallas as pl
from jax.experimental.pallas import tpu as pltpu
from jax.sharding import Mesh
from jax.sharding import PartitionSpec as P


NY = 32
NZ = 16
PLANE = NY * NZ
VOX = ("y", "zh", "x")
XY = ("y", "x")
CHAN = ("zl", "co")
F32 = jnp.float32
BF16 = jnp.bfloat16


def moved(value, b, c):
    step = NZ * b + c
    if step == 0:
        return value
    out = pltpu.roll(value, (-step) % PLANE, 1)
    lane = lax.broadcasted_iota(jnp.int32, value.shape, 1)
    keep = None
    if b != 0:
        keep = (lane + NZ * b >= 0) & (lane + NZ * b < PLANE)
    if c != 0:
        col = lane % NZ + c
        inside = (col >= 0) & (col < NZ)
        keep = inside if keep is None else keep & inside
    return jnp.where(keep, out, 0.0)


def forward_kernel(w_ref, low_ref, high_ref, o_ref, x_rows):
    rows = o_ref.shape[1]
    cores, chips, ch = low_ref.shape[:3]
    for z in range(chips):
        for e in range(cores):
            for half, ref in enumerate((low_ref, high_ref)):
                first = ((z * cores + e) * 2 + half) * ch
                x_rows[first : first + ch, :] = ref[e, z]
    for a in range(3):
        y = jnp.dot(w_ref[9 * rows * a : 9 * rows * (a + 1), :], x_rows[...], preferred_element_type=F32)
        total = None
        for b in range(3):
            for c in range(3):
                k = 3 * b + c
                term = moved(y[rows * k : rows * (k + 1), :], b - 1, c - 1)
                total = term if total is None else total + term
        o_ref[a] = total


def forward(w_rows, low, high):
    rows = w_rows.shape[0] // 27
    return pl.pallas_call(
        forward_kernel,
        out_shape=jax.ShapeDtypeStruct((3, rows, PLANE), F32),
        scratch_shapes=[pltpu.VMEM((w_rows.shape[1], PLANE), BF16)],
        compiler_params=pltpu.CompilerParams(vmem_limit_bytes=32 * 2**20),
        name="forward_plane",
    )(w_rows, low, high)


def backward_kernel(w_ref, u_ref, o_ref, cols):
    rows = u_ref.shape[1]
    for a in range(3):
        plane = u_ref[2 - a].astype(F32)
        for b in range(3):
            for c in range(3):
                k = 9 * a + 3 * b + c
                cols[rows * k : rows * (k + 1), :] = moved(plane, 1 - b, 1 - c).astype(BF16)
    ch = o_ref.shape[1]
    for t in range(o_ref.shape[0]):
        part = w_ref[:, ch * t : ch * (t + 1)]
        o_ref[t] = lax.dot_general(part, cols[...], (((0,), (0,)), ((), ())), preferred_element_type=F32)


def backward(w_rows, planes):
    width = w_rows.shape[1]
    rows = planes.shape[1]
    return pl.pallas_call(
        backward_kernel,
        out_shape=jax.ShapeDtypeStruct((width // 128, 128, PLANE), F32),
        scratch_shapes=[pltpu.VMEM((27 * rows, PLANE), BF16)],
        compiler_params=pltpu.CompilerParams(vmem_limit_bytes=32 * 2**20),
        name="backward_plane",
    )(w_rows, planes)


def filter_kernel(a_ref, u_ref, o_ref, lhs, rhs, acc):
    cores, run, chans = a_ref.shape[:3]
    rows = (u_ref.shape[1] - chans) // 2

    @pl.when(pl.program_id(0) == 0)
    def _():
        acc[...] = jnp.zeros_like(acc)

    for q in range(run + 2):
        holder = min(max(q - 1, 0), run - 1)
        first = chans if holder == q - 1 else chans + rows
        plane = u_ref[holder, first : first + rows, :].astype(F32)
        for c in range(3):
            lhs[q, rows * c : rows * (c + 1), :] = moved(plane, 0, 1 - c).astype(BF16)
    for q in range(run):
        for e in range(cores):
            plane = a_ref[e, q].astype(F32)
            for b in range(3):
                first = chans * (cores * b + e)
                rhs[q, first : first + chans, :] = moved(plane, b - 1, 0).astype(BF16)
    total = acc[...]
    for q in range(run):
        left = lhs[q : q + 3].reshape(9 * rows, PLANE)
        total = total + lax.dot_general(left, rhs[q], (((1,), (1,)), ((), ())), preferred_element_type=F32)
    acc[...] = total

    @pl.when(pl.program_id(0) == pl.num_programs(0) - 1)
    def _():
        group = lax.broadcasted_iota(jnp.int32, (8, 128), 1) // 32
        for k in range(27):
            a, b, c = k // 9, k // 3 % 3, k % 3
            for h in range(o_ref.shape[0]):
                row = rows * (3 * (2 - a) + c) + 16 * h
                sides = []
                for first in (row, row + 8):
                    if b == 2:
                        side = total[first : first + 8, 128:192]
                        side = jnp.concatenate([side, side], axis=1)
                    else:
                        side = total[first : first + 8, 0:128]
                    sides.append(pltpu.roll(side, 64, 1) if b == 1 else side)
                one, two = sides
                left = jnp.where(group == 0, one, pltpu.roll(two, 32, 1))
                right = jnp.where(group == 2, pltpu.roll(one, 32, 1), pltpu.roll(two, 64, 1))
                o_ref[h, k] = jnp.where(group < 2, left, right)


def filter_grad(acts, mixed, runs):
    cores, planes, chans = acts.shape[:3]
    height = mixed.shape[1]
    rows = (height - chans) // 2
    run = planes // runs
    return pl.pallas_call(
        filter_kernel,
        grid=(runs,),
        in_specs=[
            pl.BlockSpec((cores, run, chans, PLANE), lambda r: (0, r, 0, 0)),
            pl.BlockSpec((run, height, PLANE), lambda r: (r, 0, 0)),
        ],
        out_specs=pl.BlockSpec((rows // 16, 27, 8, 128), lambda r: (0, 0, 0, 0)),
        out_shape=jax.ShapeDtypeStruct((rows // 16, 27, 8, 128), F32),
        scratch_shapes=[
            pltpu.VMEM((run + 2, 3 * rows, PLANE), BF16),
            pltpu.VMEM((run, 3 * cores * chans, PLANE), BF16),
            pltpu.VMEM((9 * rows, 3 * cores * chans), F32),
        ],
        compiler_params=pltpu.CompilerParams(vmem_limit_bytes=32 * 2**20),
        name="filter_planes",
    )(acts, mixed)


def join_kernel(r_ref, o_ref):
    even = lax.broadcasted_iota(jnp.int32, (8, 128), 1) // 32 % 2 == 0
    for k in range(o_ref.shape[0]):
        for t in range(r_ref.shape[0] // 2):
            for h in range(r_ref.shape[1]):
                left = r_ref[2 * t, h, k].astype(F32)
                right = r_ref[2 * t + 1, h, k].astype(F32)
                one = jnp.where(even, left, pltpu.roll(right, 32, 1))
                two = jnp.where(even, pltpu.roll(left, 96, 1), right)
                both = jnp.concatenate([one, two], axis=0).astype(BF16)
                o_ref[k, 16 * h : 16 * (h + 1), 128 * t : 128 * (t + 1)] = both


def join(pieces):
    size, halves = pieces.shape[:2]
    return pl.pallas_call(
        join_kernel,
        grid=(3,),
        in_specs=[pl.BlockSpec((size, halves, 9, 8, 128), lambda g: (0, 0, g, 0, 0))],
        out_specs=pl.BlockSpec((9, 16 * halves, 64 * size), lambda g: (g, 0, 0)),
        out_shape=jax.ShapeDtypeStruct((27, 16 * halves, 64 * size), BF16),
        compiler_params=pltpu.CompilerParams(vmem_limit_bytes=16 * 2**20),
        name="join_pieces",
    )(pieces)


def exchange(pieces, axes):
    return lax.all_to_all(pieces, axes, 0, 0, tiled=True)


def shared(value, axes):
    return exchange(jnp.broadcast_to(value, (lax.axis_size(axes), *value.shape)), axes)


def local(activations, upstream, weights):
    ch, co = activations.shape[0], upstream.shape[0]
    n_vox, n_y = lax.axis_size(VOX), lax.axis_size("y")
    n_xy, n_chan = lax.axis_size(XY), lax.axis_size(CHAN)
    cin = ch * n_chan
    up = [(i, i + 1) for i in range(n_vox - 1)]
    down = [(i + 1, i) for i in range(n_vox - 1)]
    act = activations.reshape(ch, PLANE)
    ups = upstream.reshape(co, PLANE)

    before = lax.ppermute(ups, VOX, up)
    after = lax.ppermute(ups, VOX, down)

    near = shared(act, "zl")

    w_rows = weights.transpose(1, 0, 2).reshape(27 * co, cin)
    part = backward(w_rows, jnp.stack([before, ups, after]))
    part = lax.psum_scatter(part.reshape(cin, PLANE), CHAN, scatter_dimension=0, tiled=True)
    input_grad = part.astype(BF16).reshape(ch, 1, PLANE)

    edge = jnp.where(lax.axis_index("x") == 0, before, after)
    planes = jnp.broadcast_to(jnp.concatenate([ups, edge]), (n_xy, 2 * co, PLANE))
    mixed = jnp.concatenate([near.reshape(n_xy, cin // (2 * n_xy), PLANE), planes], axis=1)
    mixed = exchange(mixed, XY)

    low = lax.all_gather(near[:, : ch // 2], "co", axis=0, tiled=False)
    high = lax.all_gather(near[:, ch // 2 :], "co", axis=0, tiled=False)
    around = forward(w_rows, low, high)
    after_part = lax.ppermute(around[2], VOX, down)
    before_part = lax.ppermute(around[0], VOX, up)
    outputs = (around[1] + after_part + before_part).astype(BF16).reshape(co, 1, PLANE)

    acts = shared(mixed[:, : cin // (2 * n_xy)], "co")
    raw = filter_grad(acts, mixed, n_y)
    raw = exchange(raw, "zh")
    raw = jnp.sum(raw, axis=0)
    scale = 1.0 / jnp.sqrt(jnp.float32(n_vox * PLANE))
    mine = (raw * scale).astype(BF16)
    halves = shared(mine, "zh")
    pieces = shared(halves, XY)
    weight_grad = join(pieces).transpose(1, 0, 2)
    return (outputs, input_grad, weight_grad)


def solution(mesh):
    finer = Mesh(mesh.devices.reshape(SPLIT), ("y", "zh", "x", "zl", "co"))
    specs = (P(CHAN, VOX, None), P(CHAN, VOX, None), P(CHAN, None, None))

    return jax.shard_map(local, mesh=finer, in_specs=specs, out_specs=specs, check_vma=False)


SPLIT = (4, 2, 4, 8, 2)
```

```python
import jax
import jax.numpy as jnp
from jax import lax
from jax.experimental import pallas as pl
from jax.experimental.pallas import tpu as pltpu
from jax.sharding import Mesh
from jax.sharding import PartitionSpec as P


NY = 32
NZ = 16
PLANE = NY * NZ
VOX = ("y", "zh", "x")
XY = ("y", "x")
CHAN = ("zl", "co")
F32 = jnp.float32
BF16 = jnp.bfloat16


def moved(value, b, c):
    step = NZ * b + c
    if step == 0:
        return value
    out = pltpu.roll(value, (-step) % PLANE, 1)
    lane = lax.broadcasted_iota(jnp.int32, value.shape, 1)
    keep = None
    if b != 0:
        keep = (lane + NZ * b >= 0) & (lane + NZ * b < PLANE)
    if c != 0:
        col = lane % NZ + c
        inside = (col >= 0) & (col < NZ)
        keep = inside if keep is None else keep & inside
    return jnp.where(keep, out, 0.0)


def forward_kernel(w_ref, low_ref, high_ref, o_ref, x_rows):
    rows = o_ref.shape[1]
    cores, chips, ch = low_ref.shape[:3]
    for z in range(chips):
        for e in range(cores):
            for half, ref in enumerate((low_ref, high_ref)):
                first = ((z * cores + e) * 2 + half) * ch
                x_rows[first : first + ch, :] = ref[e, z]
    for a in range(3):
        y = jnp.dot(w_ref[9 * rows * a : 9 * rows * (a + 1), :], x_rows[...], preferred_element_type=F32)
        total = None
        for b in range(3):
            for c in range(3):
                k = 3 * b + c
                term = moved(y[rows * k : rows * (k + 1), :], b - 1, c - 1)
                total = term if total is None else total + term
        o_ref[a] = total


def forward(w_rows, low, high):
    rows = w_rows.shape[0] // 27
    return pl.pallas_call(
        forward_kernel,
        out_shape=jax.ShapeDtypeStruct((3, rows, PLANE), F32),
        scratch_shapes=[pltpu.VMEM((w_rows.shape[1], PLANE), BF16)],
        compiler_params=pltpu.CompilerParams(vmem_limit_bytes=32 * 2**20),
        name="forward_plane",
    )(w_rows, low, high)


def backward_kernel(w_ref, u_ref, o_ref, cols):
    rows = u_ref.shape[1]
    for a in range(3):
        plane = u_ref[2 - a].astype(F32)
        for b in range(3):
            for c in range(3):
                k = 9 * a + 3 * b + c
                cols[rows * k : rows * (k + 1), :] = moved(plane, 1 - b, 1 - c).astype(BF16)
    cores, chips, ch = o_ref.shape[:3]
    for t in range(chips):
        part = w_ref[:, cores * ch * t : cores * ch * (t + 1)]
        got = lax.dot_general(part, cols[...], (((0,), (0,)), ((), ())), preferred_element_type=F32)
        for e in range(cores):
            o_ref[e, t] = got[ch * e : ch * (e + 1)]


def backward(w_rows, planes, cores, chips):
    width = w_rows.shape[1]
    rows = planes.shape[1]
    return pl.pallas_call(
        backward_kernel,
        out_shape=jax.ShapeDtypeStruct((cores, chips, width // (cores * chips), PLANE), F32),
        scratch_shapes=[pltpu.VMEM((27 * rows, PLANE), BF16)],
        compiler_params=pltpu.CompilerParams(vmem_limit_bytes=32 * 2**20),
        name="backward_plane",
    )(w_rows, planes)


def filter_kernel(a_ref, u_ref, o_ref, lhs, rhs, acc):
    cores, run, chans = a_ref.shape[:3]
    rows = (u_ref.shape[1] - chans) // 2

    @pl.when(pl.program_id(0) == 0)
    def _():
        acc[...] = jnp.zeros_like(acc)

    for q in range(run + 2):
        holder = min(max(q - 1, 0), run - 1)
        first = chans if holder == q - 1 else chans + rows
        plane = u_ref[holder, first : first + rows, :].astype(F32)
        for c in range(3):
            lhs[q, rows * c : rows * (c + 1), :] = moved(plane, 0, 1 - c).astype(BF16)
    for q in range(run):
        for e in range(cores):
            plane = a_ref[e, q].astype(F32)
            for b in range(3):
                first = chans * (cores * b + e)
                rhs[q, first : first + chans, :] = moved(plane, b - 1, 0).astype(BF16)
    total = acc[...]
    for q in range(run):
        left = lhs[q : q + 3].reshape(9 * rows, PLANE)
        total = total + lax.dot_general(left, rhs[q], (((1,), (1,)), ((), ())), preferred_element_type=F32)
    acc[...] = total

    @pl.when(pl.program_id(0) == pl.num_programs(0) - 1)
    def _():
        group = lax.broadcasted_iota(jnp.int32, (8, 128), 1) // 32
        for k in range(27):
            a, b, c = k // 9, k // 3 % 3, k % 3
            for h in range(o_ref.shape[0]):
                row = rows * (3 * (2 - a) + c) + 16 * h
                sides = []
                for first in (row, row + 8):
                    if b == 2:
                        side = total[first : first + 8, 128:192]
                        side = jnp.concatenate([side, side], axis=1)
                    else:
                        side = total[first : first + 8, 0:128]
                    sides.append(pltpu.roll(side, 64, 1) if b == 1 else side)
                one, two = sides
                left = jnp.where(group == 0, one, pltpu.roll(two, 32, 1))
                right = jnp.where(group == 2, pltpu.roll(one, 32, 1), pltpu.roll(two, 64, 1))
                o_ref[h, k] = jnp.where(group < 2, left, right)


def filter_grad(acts, mixed, runs):
    cores, planes, chans = acts.shape[:3]
    height = mixed.shape[1]
    rows = (height - chans) // 2
    run = planes // runs
    return pl.pallas_call(
        filter_kernel,
        grid=(runs,),
        in_specs=[
            pl.BlockSpec((cores, run, chans, PLANE), lambda r: (0, r, 0, 0)),
            pl.BlockSpec((run, height, PLANE), lambda r: (r, 0, 0)),
        ],
        out_specs=pl.BlockSpec((rows // 16, 27, 8, 128), lambda r: (0, 0, 0, 0)),
        out_shape=jax.ShapeDtypeStruct((rows // 16, 27, 8, 128), F32),
        scratch_shapes=[
            pltpu.VMEM((run + 2, 3 * rows, PLANE), BF16),
            pltpu.VMEM((run, 3 * cores * chans, PLANE), BF16),
            pltpu.VMEM((9 * rows, 3 * cores * chans), F32),
        ],
        compiler_params=pltpu.CompilerParams(vmem_limit_bytes=32 * 2**20),
        name="filter_planes",
    )(acts, mixed)


def join_kernel(r_ref, o_ref):
    even = lax.broadcasted_iota(jnp.int32, (8, 128), 1) // 32 % 2 == 0
    for k in range(o_ref.shape[0]):
        for t in range(r_ref.shape[0] // 2):
            for h in range(r_ref.shape[1]):
                left = r_ref[2 * t, h, k].astype(F32)
                right = r_ref[2 * t + 1, h, k].astype(F32)
                one = jnp.where(even, left, pltpu.roll(right, 32, 1))
                two = jnp.where(even, pltpu.roll(left, 96, 1), right)
                both = jnp.concatenate([one, two], axis=0).astype(BF16)
                o_ref[k, 16 * h : 16 * (h + 1), 128 * t : 128 * (t + 1)] = both


def join(pieces):
    size, halves = pieces.shape[:2]
    return pl.pallas_call(
        join_kernel,
        grid=(3,),
        in_specs=[pl.BlockSpec((size, halves, 9, 8, 128), lambda g: (0, 0, g, 0, 0))],
        out_specs=pl.BlockSpec((9, 16 * halves, 64 * size), lambda g: (g, 0, 0)),
        out_shape=jax.ShapeDtypeStruct((27, 16 * halves, 64 * size), BF16),
        compiler_params=pltpu.CompilerParams(vmem_limit_bytes=16 * 2**20),
        name="join_pieces",
    )(pieces)


def exchange(pieces, axes):
    return lax.all_to_all(pieces, axes, 0, 0, tiled=True)


def shared(value, axes):
    return exchange(jnp.broadcast_to(value, (lax.axis_size(axes), *value.shape)), axes)


def local(activations, upstream, weights):
    ch, co = activations.shape[0], upstream.shape[0]
    n_vox, n_y = lax.axis_size(VOX), lax.axis_size("y")
    n_xy, n_chan = lax.axis_size(XY), lax.axis_size(CHAN)
    cin = ch * n_chan
    up = [(i, i + 1) for i in range(n_vox - 1)]
    down = [(i + 1, i) for i in range(n_vox - 1)]
    act = activations.reshape(ch, PLANE)
    ups = upstream.reshape(co, PLANE)

    before = lax.ppermute(ups, VOX, up)
    after = lax.ppermute(ups, VOX, down)

    near = shared(act, "zl")

    w_rows = weights.transpose(1, 0, 2).reshape(27 * co, cin)
    part = backward(w_rows, jnp.stack([before, ups, after]), lax.axis_size("co"), lax.axis_size("zl"))
    part = lax.psum_scatter(part.reshape(cin, PLANE), "co", scatter_dimension=0, tiled=True)
    part = lax.psum_scatter(part, "zl", scatter_dimension=0, tiled=True)
    input_grad = part.astype(BF16).reshape(ch, 1, PLANE)

    edge = jnp.where(lax.axis_index("x") == 0, before, after)
    planes = jnp.broadcast_to(jnp.concatenate([ups, edge]), (n_xy, 2 * co, PLANE))
    mixed = jnp.concatenate([near.reshape(n_xy, cin // (2 * n_xy), PLANE), planes], axis=1)
    mixed = exchange(mixed, XY)

    low = lax.all_gather(near[:, : ch // 2], "co", axis=0, tiled=False)
    high = lax.all_gather(near[:, ch // 2 :], "co", axis=0, tiled=False)
    around = forward(w_rows, low, high)
    after_part = lax.ppermute(around[2], VOX, down)
    before_part = lax.ppermute(around[0], VOX, up)
    outputs = (around[1] + after_part + before_part).astype(BF16).reshape(co, 1, PLANE)

    acts = shared(mixed[:, : cin // (2 * n_xy)], "co")
    raw = filter_grad(acts, mixed, n_y)
    raw = exchange(raw, "zh")
    raw = jnp.sum(raw, axis=0)
    scale = 1.0 / jnp.sqrt(jnp.float32(n_vox * PLANE))
    mine = (raw * scale).astype(BF16)
    halves = shared(mine, "zh")
    pieces = shared(halves, XY)
    weight_grad = join(pieces).transpose(1, 0, 2)
    return (outputs, input_grad, weight_grad)


def solution(mesh):
    finer = Mesh(mesh.devices.reshape(SPLIT), ("y", "zh", "x", "zl", "co"))
    specs = (P(CHAN, VOX, None), P(CHAN, VOX, None), P(CHAN, None, None))

    return jax.shard_map(local, mesh=finer, in_specs=specs, out_specs=specs, check_vma=False)


SPLIT = (4, 2, 4, 8, 2)
```

```python
import jax
import jax.numpy as jnp
from jax import lax
from jax.experimental import pallas as pl
from jax.experimental.pallas import tpu as pltpu
from jax.sharding import Mesh
from jax.sharding import PartitionSpec as P


NY = 32
NZ = 16
PLANE = NY * NZ
VOX = ("y", "zh", "x")
XY = ("y", "x")
CHAN = ("zl", "co")
F32 = jnp.float32
BF16 = jnp.bfloat16


def moved(value, b, c):
    step = NZ * b + c
    if step == 0:
        return value
    out = pltpu.roll(value, (-step) % PLANE, 1)
    lane = lax.broadcasted_iota(jnp.int32, value.shape, 1)
    keep = None
    if b != 0:
        keep = (lane + NZ * b >= 0) & (lane + NZ * b < PLANE)
    if c != 0:
        col = lane % NZ + c
        inside = (col >= 0) & (col < NZ)
        keep = inside if keep is None else keep & inside
    return jnp.where(keep, out, 0.0)


def forward_kernel(w_ref, low_ref, high_ref, o_ref, x_rows):
    rows = o_ref.shape[1]
    cores, chips, ch = low_ref.shape[:3]
    for z in range(chips):
        for e in range(cores):
            for half, ref in enumerate((low_ref, high_ref)):
                first = ((z * cores + e) * 2 + half) * ch
                x_rows[first : first + ch, :] = ref[e, z]
    for a in range(3):
        y = jnp.dot(w_ref[9 * rows * a : 9 * rows * (a + 1), :], x_rows[...], preferred_element_type=F32)
        total = None
        for b in range(3):
            for c in range(3):
                k = 3 * b + c
                term = moved(y[rows * k : rows * (k + 1), :], b - 1, c - 1)
                total = term if total is None else total + term
        o_ref[a] = total


def forward(w_rows, low, high):
    rows = w_rows.shape[0] // 27
    return pl.pallas_call(
        forward_kernel,
        out_shape=jax.ShapeDtypeStruct((3, rows, PLANE), F32),
        scratch_shapes=[pltpu.VMEM((w_rows.shape[1], PLANE), BF16)],
        compiler_params=pltpu.CompilerParams(vmem_limit_bytes=32 * 2**20),
        name="forward_plane",
    )(w_rows, low, high)


def backward_kernel(w_ref, u_ref, o_ref, cols):
    rows = u_ref.shape[1]
    for a in range(3):
        plane = u_ref[2 - a].astype(F32)
        for b in range(3):
            for c in range(3):
                k = 9 * a + 3 * b + c
                cols[rows * k : rows * (k + 1), :] = moved(plane, 1 - b, 1 - c).astype(BF16)
    cores, chips, ch = o_ref.shape[:3]
    for t in range(chips):
        part = w_ref[:, cores * ch * t : cores * ch * (t + 1)]
        got = lax.dot_general(part, cols[...], (((0,), (0,)), ((), ())), preferred_element_type=F32)
        for e in range(cores):
            o_ref[e, t] = got[ch * e : ch * (e + 1)]


def backward(w_rows, planes, cores, chips):
    width = w_rows.shape[1]
    rows = planes.shape[1]
    return pl.pallas_call(
        backward_kernel,
        out_shape=jax.ShapeDtypeStruct((cores, chips, width // (cores * chips), PLANE), F32),
        scratch_shapes=[pltpu.VMEM((27 * rows, PLANE), BF16)],
        compiler_params=pltpu.CompilerParams(vmem_limit_bytes=32 * 2**20),
        name="backward_plane",
    )(w_rows, planes)


def filter_kernel(a_ref, u_ref, o_ref, lhs, rhs, acc):
    cores, run, chans = a_ref.shape[:3]
    rows = (u_ref.shape[1] - chans) // 2

    @pl.when(pl.program_id(0) == 0)
    def _():
        acc[...] = jnp.zeros_like(acc)

    for q in range(run + 2):
        holder = min(max(q - 1, 0), run - 1)
        first = chans if holder == q - 1 else chans + rows
        plane = u_ref[holder, first : first + rows, :].astype(F32)
        for c in range(3):
            lhs[q, rows * c : rows * (c + 1), :] = moved(plane, 0, 1 - c).astype(BF16)
    for q in range(run):
        for e in range(cores):
            plane = a_ref[e, q].astype(F32)
            for b in range(3):
                first = chans * (cores * b + e)
                rhs[q, first : first + chans, :] = moved(plane, b - 1, 0).astype(BF16)
    total = acc[...]
    for q in range(run):
        left = lhs[q : q + 3].reshape(9 * rows, PLANE)
        total = total + lax.dot_general(left, rhs[q], (((1,), (1,)), ((), ())), preferred_element_type=F32)
    acc[...] = total

    @pl.when(pl.program_id(0) == pl.num_programs(0) - 1)
    def _():
        group = lax.broadcasted_iota(jnp.int32, (8, 128), 1) // 32
        for k in range(27):
            a, b, c = k // 9, k // 3 % 3, k % 3
            for h in range(o_ref.shape[0]):
                row = rows * (3 * (2 - a) + c) + 16 * h
                sides = []
                for first in (row, row + 8):
                    if b == 2:
                        side = total[first : first + 8, 128:192]
                        side = jnp.concatenate([side, side], axis=1)
                    else:
                        side = total[first : first + 8, 0:128]
                    sides.append(pltpu.roll(side, 64, 1) if b == 1 else side)
                one, two = sides
                left = jnp.where(group == 0, one, pltpu.roll(two, 32, 1))
                right = jnp.where(group == 2, pltpu.roll(one, 32, 1), pltpu.roll(two, 64, 1))
                o_ref[h, k] = jnp.where(group < 2, left, right)


def filter_grad(acts, mixed, runs):
    cores, planes, chans = acts.shape[:3]
    height = mixed.shape[1]
    rows = (height - chans) // 2
    run = planes // runs
    return pl.pallas_call(
        filter_kernel,
        grid=(runs,),
        in_specs=[
            pl.BlockSpec((cores, run, chans, PLANE), lambda r: (0, r, 0, 0)),
            pl.BlockSpec((run, height, PLANE), lambda r: (r, 0, 0)),
        ],
        out_specs=pl.BlockSpec((rows // 16, 27, 8, 128), lambda r: (0, 0, 0, 0)),
        out_shape=jax.ShapeDtypeStruct((rows // 16, 27, 8, 128), F32),
        scratch_shapes=[
            pltpu.VMEM((run + 2, 3 * rows, PLANE), BF16),
            pltpu.VMEM((run, 3 * cores * chans, PLANE), BF16),
            pltpu.VMEM((9 * rows, 3 * cores * chans), F32),
        ],
        compiler_params=pltpu.CompilerParams(vmem_limit_bytes=32 * 2**20),
        name="filter_planes",
    )(acts, mixed)


def join_kernel(own_ref, a_ref, b_ref, o_ref):
    even = lax.broadcasted_iota(jnp.int32, (8, 128), 1) // 32 % 2 == 0
    for ref, side in ((a_ref, own_ref[0]), (b_ref, 1 - own_ref[0])):
        first = pl.multiple_of(16 * side, 16)
        for k in range(o_ref.shape[0]):
            for t in range(ref.shape[0] // 2):
                left = ref[2 * t, k].astype(F32)
                right = ref[2 * t + 1, k].astype(F32)
                one = jnp.where(even, left, pltpu.roll(right, 32, 1))
                two = jnp.where(even, pltpu.roll(left, 96, 1), right)
                both = jnp.concatenate([one, two], axis=0).astype(BF16)
                o_ref[k, pl.ds(first, 16), 128 * t : 128 * (t + 1)] = both


def join(own, pieces, others):
    size = pieces.shape[0]
    block = pl.BlockSpec((size, 9, 8, 128), lambda g, own: (0, g, 0, 0))
    return pl.pallas_call(
        join_kernel,
        grid_spec=pltpu.PrefetchScalarGridSpec(
            num_scalar_prefetch=1,
            grid=(3,),
            in_specs=[block, block],
            out_specs=pl.BlockSpec((9, 32, 64 * size), lambda g, own: (g, 0, 0)),
        ),
        out_shape=jax.ShapeDtypeStruct((27, 32, 64 * size), BF16),
        compiler_params=pltpu.CompilerParams(vmem_limit_bytes=16 * 2**20),
        name="join_pieces",
    )(own, pieces, others)


def exchange(pieces, axes):
    return lax.all_to_all(pieces, axes, 0, 0, tiled=True)


def shared(value, axes):
    return exchange(jnp.broadcast_to(value, (lax.axis_size(axes), *value.shape)), axes)


def local(activations, upstream, weights):
    ch, co = activations.shape[0], upstream.shape[0]
    n_vox, n_y = lax.axis_size(VOX), lax.axis_size("y")
    n_xy, n_chan = lax.axis_size(XY), lax.axis_size(CHAN)
    cin = ch * n_chan
    up = [(i, i + 1) for i in range(n_vox - 1)]
    down = [(i + 1, i) for i in range(n_vox - 1)]
    act = activations.reshape(ch, PLANE)
    ups = upstream.reshape(co, PLANE)

    before = lax.ppermute(ups, VOX, up)
    after = lax.ppermute(ups, VOX, down)

    near = shared(act, "zl")

    w_rows = weights.transpose(1, 0, 2).reshape(27 * co, cin)
    part = backward(w_rows, jnp.stack([before, ups, after]), lax.axis_size("co"), lax.axis_size("zl"))
    part = lax.psum_scatter(part.reshape(cin, PLANE), "co", scatter_dimension=0, tiled=True)
    part = lax.psum_scatter(part, "zl", scatter_dimension=0, tiled=True)
    input_grad = part.astype(BF16).reshape(ch, 1, PLANE)

    edge = jnp.where(lax.axis_index("x") == 0, before, after)
    planes = jnp.broadcast_to(jnp.concatenate([ups, edge]), (n_xy, 2 * co, PLANE))
    mixed = jnp.concatenate([near.reshape(n_xy, cin // (2 * n_xy), PLANE), planes], axis=1)
    mixed = exchange(mixed, XY)

    low = lax.all_gather(near[:, : ch // 2], "co", axis=0, tiled=False)
    high = lax.all_gather(near[:, ch // 2 :], "co", axis=0, tiled=False)
    around = forward(w_rows, low, high)
    after_part = lax.ppermute(around[2], VOX, down)
    before_part = lax.ppermute(around[0], VOX, up)
    outputs = (around[1] + after_part + before_part).astype(BF16).reshape(co, 1, PLANE)

    low_acts = mixed[:, : cin // (2 * n_xy)]
    acts = shared(low_acts, "co")
    raw = filter_grad(acts, mixed, n_y)
    raw = exchange(raw, "zh")
    raw = jnp.sum(raw, axis=0)
    scale = 1.0 / jnp.sqrt(jnp.float32(n_vox * PLANE))
    mine = (raw * scale).astype(BF16)
    pieces = shared(mine, XY)
    other = lax.ppermute(mine, "zh", [(0, 1), (1, 0)])
    others = shared(other, XY)
    weight_grad = join(lax.axis_index("zh").reshape(1), pieces, others).transpose(1, 0, 2)
    return (outputs, input_grad, weight_grad)


def solution(mesh):
    finer = Mesh(mesh.devices.reshape(SPLIT), ("y", "zh", "x", "zl", "co"))
    specs = (P(CHAN, VOX, None), P(CHAN, VOX, None), P(CHAN, None, None))

    return jax.shard_map(local, mesh=finer, in_specs=specs, out_specs=specs, check_vma=False)


SPLIT = (4, 2, 4, 8, 2)
```

```python
import jax
import jax.numpy as jnp
from jax import lax
from jax.experimental import pallas as pl
from jax.experimental.pallas import tpu as pltpu
from jax.sharding import Mesh
from jax.sharding import PartitionSpec as P


NY = 32
NZ = 16
PLANE = NY * NZ
VOX = ("y", "zh", "x")
XY = ("y", "x")
CHAN = ("zl", "co")
RING = ("zh", "zl")
F32 = jnp.float32
BF16 = jnp.bfloat16


def moved(value, b, c):
    step = NZ * b + c
    if step == 0:
        return value
    out = pltpu.roll(value, (-step) % PLANE, 1)
    lane = lax.broadcasted_iota(jnp.int32, value.shape, 1)
    keep = None
    if b != 0:
        keep = (lane + NZ * b >= 0) & (lane + NZ * b < PLANE)
    if c != 0:
        col = lane % NZ + c
        inside = (col >= 0) & (col < NZ)
        keep = inside if keep is None else keep & inside
    return jnp.where(keep, out, 0.0)


def forward_kernel(w_ref, low_ref, high_ref, o_ref, x_rows):
    rows = o_ref.shape[1]
    cores, chips, ch = low_ref.shape[:3]
    for z in range(chips):
        for e in range(cores):
            for half, ref in enumerate((low_ref, high_ref)):
                first = ((z * cores + e) * 2 + half) * ch
                x_rows[first : first + ch, :] = ref[e, z]
    for a in range(3):
        y = jnp.dot(w_ref[9 * rows * a : 9 * rows * (a + 1), :], x_rows[...], preferred_element_type=F32)
        total = None
        for b in range(3):
            for c in range(3):
                k = 3 * b + c
                term = moved(y[rows * k : rows * (k + 1), :], b - 1, c - 1)
                total = term if total is None else total + term
        o_ref[a] = total


def forward(w_rows, low, high):
    rows = w_rows.shape[0] // 27
    return pl.pallas_call(
        forward_kernel,
        out_shape=jax.ShapeDtypeStruct((3, rows, PLANE), F32),
        scratch_shapes=[pltpu.VMEM((w_rows.shape[1], PLANE), BF16)],
        compiler_params=pltpu.CompilerParams(vmem_limit_bytes=32 * 2**20),
        name="forward_plane",
    )(w_rows, low, high)


def backward_kernel(w_ref, u_ref, o_ref, cols):
    rows = u_ref.shape[1]
    for a in range(3):
        plane = u_ref[2 - a].astype(F32)
        for b in range(3):
            for c in range(3):
                k = 9 * a + 3 * b + c
                cols[rows * k : rows * (k + 1), :] = moved(plane, 1 - b, 1 - c).astype(BF16)
    cores, chips, ch = o_ref.shape[:3]
    for t in range(chips):
        part = w_ref[:, cores * ch * t : cores * ch * (t + 1)]
        got = lax.dot_general(part, cols[...], (((0,), (0,)), ((), ())), preferred_element_type=F32)
        for e in range(cores):
            o_ref[e, t] = got[ch * e : ch * (e + 1)]


def backward(w_rows, planes, cores, chips):
    width = w_rows.shape[1]
    rows = planes.shape[1]
    return pl.pallas_call(
        backward_kernel,
        out_shape=jax.ShapeDtypeStruct((cores, chips, width // (cores * chips), PLANE), F32),
        scratch_shapes=[pltpu.VMEM((27 * rows, PLANE), BF16)],
        compiler_params=pltpu.CompilerParams(vmem_limit_bytes=32 * 2**20),
        name="backward_plane",
    )(w_rows, planes)


def filter_kernel(a_ref, u_ref, o_ref, lhs, rhs, acc):
    cores, run, chans = a_ref.shape[:3]
    rows = (u_ref.shape[1] - chans) // 2

    @pl.when(pl.program_id(0) == 0)
    def _():
        acc[...] = jnp.zeros_like(acc)

    for q in range(run + 2):
        holder = min(max(q - 1, 0), run - 1)
        first = chans if holder == q - 1 else chans + rows
        plane = u_ref[holder, first : first + rows, :].astype(F32)
        for c in range(3):
            lhs[q, rows * c : rows * (c + 1), :] = moved(plane, 0, 1 - c).astype(BF16)
    for q in range(run):
        for e in range(cores):
            plane = a_ref[e, q].astype(F32)
            for b in range(3):
                first = chans * (cores * b + e)
                rhs[q, first : first + chans, :] = moved(plane, b - 1, 0).astype(BF16)
    total = acc[...]
    for q in range(run):
        left = lhs[q : q + 3].reshape(9 * rows, PLANE)
        total = total + lax.dot_general(left, rhs[q], (((1,), (1,)), ((), ())), preferred_element_type=F32)
    acc[...] = total

    @pl.when(pl.program_id(0) == pl.num_programs(0) - 1)
    def _():
        group = lax.broadcasted_iota(jnp.int32, (8, 128), 1) // 32
        for k in range(27):
            a, b, c = k // 9, k // 3 % 3, k % 3
            for h in range(o_ref.shape[0]):
                row = rows * (3 * (2 - a) + c) + 16 * h
                sides = []
                for first in (row, row + 8):
                    if b == 2:
                        side = total[first : first + 8, 128:192]
                        side = jnp.concatenate([side, side], axis=1)
                    else:
                        side = total[first : first + 8, 0:128]
                    sides.append(pltpu.roll(side, 64, 1) if b == 1 else side)
                one, two = sides
                left = jnp.where(group == 0, one, pltpu.roll(two, 32, 1))
                right = jnp.where(group == 2, pltpu.roll(one, 32, 1), pltpu.roll(two, 64, 1))
                o_ref[h, k] = jnp.where(group < 2, left, right)


def filter_grad(acts, mixed, runs):
    cores, planes, chans = acts.shape[:3]
    height = mixed.shape[1]
    rows = (height - chans) // 2
    run = planes // runs
    return pl.pallas_call(
        filter_kernel,
        grid=(runs,),
        in_specs=[
            pl.BlockSpec((cores, run, chans, PLANE), lambda r: (0, r, 0, 0)),
            pl.BlockSpec((run, height, PLANE), lambda r: (r, 0, 0)),
        ],
        out_specs=pl.BlockSpec((rows // 16, 27, 8, 128), lambda r: (0, 0, 0, 0)),
        out_shape=jax.ShapeDtypeStruct((rows // 16, 27, 8, 128), F32),
        scratch_shapes=[
            pltpu.VMEM((run + 2, 3 * rows, PLANE), BF16),
            pltpu.VMEM((run, 3 * cores * chans, PLANE), BF16),
            pltpu.VMEM((9 * rows, 3 * cores * chans), F32),
        ],
        compiler_params=pltpu.CompilerParams(vmem_limit_bytes=32 * 2**20),
        name="filter_planes",
    )(acts, mixed)


def join_kernel(r_ref, o_ref):
    even = lax.broadcasted_iota(jnp.int32, (8, 128), 1) // 32 % 2 == 0
    for k in range(o_ref.shape[0]):
        for t in range(r_ref.shape[0] // 2):
            for h in range(r_ref.shape[1]):
                left = r_ref[2 * t, h, k].astype(F32)
                right = r_ref[2 * t + 1, h, k].astype(F32)
                one = jnp.where(even, left, pltpu.roll(right, 32, 1))
                two = jnp.where(even, pltpu.roll(left, 96, 1), right)
                both = jnp.concatenate([one, two], axis=0).astype(BF16)
                o_ref[k, 16 * h : 16 * (h + 1), 128 * t : 128 * (t + 1)] = both


def join(pieces):
    size, halves = pieces.shape[:2]
    return pl.pallas_call(
        join_kernel,
        grid=(3,),
        in_specs=[pl.BlockSpec((size, halves, 9, 8, 128), lambda g: (0, 0, g, 0, 0))],
        out_specs=pl.BlockSpec((9, 16 * halves, 64 * size), lambda g: (g, 0, 0)),
        out_shape=jax.ShapeDtypeStruct((27, 16 * halves, 64 * size), BF16),
        compiler_params=pltpu.CompilerParams(vmem_limit_bytes=16 * 2**20),
        name="join_pieces",
    )(pieces)


def exchange(pieces, axes):
    return lax.all_to_all(pieces, axes, 0, 0, tiled=True)


def shared(value, axes):
    return exchange(jnp.broadcast_to(value, (lax.axis_size(axes), *value.shape)), axes)


def local(activations, upstream, weights):
    ch, co = activations.shape[0], upstream.shape[0]
    n_vox, n_y = lax.axis_size(VOX), lax.axis_size("y")
    n_xy, n_chan = lax.axis_size(XY), lax.axis_size(CHAN)
    cin = ch * n_chan
    up = [(i, i + 1) for i in range(n_vox - 1)]
    down = [(i + 1, i) for i in range(n_vox - 1)]
    act = activations.reshape(ch, PLANE)
    ups = upstream.reshape(co, PLANE)

    before = lax.ppermute(ups, VOX, up)
    after = lax.ppermute(ups, VOX, down)

    near = shared(act, "zl")

    w_rows = weights.transpose(1, 0, 2).reshape(27 * co, cin)
    part = backward(w_rows, jnp.stack([before, ups, after]), lax.axis_size("co"), lax.axis_size("zl"))
    part = lax.psum_scatter(part.reshape(cin, PLANE), "co", scatter_dimension=0, tiled=True)
    part = lax.psum_scatter(part, "zl", scatter_dimension=0, tiled=True)
    input_grad = part.astype(BF16).reshape(ch, 1, PLANE)

    edge = jnp.where(lax.axis_index("x") == 0, before, after)
    planes = jnp.broadcast_to(jnp.concatenate([ups, edge]), (n_xy, 2 * co, PLANE))
    mixed = jnp.concatenate([near.reshape(n_xy, cin // (2 * n_xy), PLANE), planes], axis=1)
    mixed = exchange(mixed, XY)

    low = lax.all_gather(near[:, : ch // 2], "co", axis=0, tiled=False)
    high = lax.all_gather(near[:, ch // 2 :], "co", axis=0, tiled=False)
    around = forward(w_rows, low, high)
    after_part = lax.ppermute(around[2], VOX, down)
    before_part = lax.ppermute(around[0], VOX, up)
    outputs = (around[1] + after_part + before_part).astype(BF16).reshape(co, 1, PLANE)

    acts = shared(mixed[:, : cin // (2 * n_xy)], "co")
    raw = filter_grad(acts, mixed, n_y)
    side = lax.axis_index("zh")
    swapped = exchange(raw[:, :18], "zh")
    n_z = lax.axis_size(RING)
    back = [(i, (i - n_z // 4) % n_z) for i in range(n_z)]
    kept = jnp.where(side == 0, raw[0, 18:], raw[1, 18:])
    sent = jnp.where(side == 0, raw[1, 18:], raw[0, 18:])
    sent = lax.ppermute(sent, RING, back)
    sent = lax.ppermute(sent, RING, back)
    swapped = jnp.sum(swapped, axis=0)
    raw = jnp.concatenate([swapped, kept + sent])
    scale = 1.0 / jnp.sqrt(jnp.float32(n_vox * PLANE))
    mine = (raw * scale).astype(BF16)
    halves = shared(mine, "zh")
    pieces = shared(halves, XY)
    weight_grad = join(pieces).transpose(1, 0, 2)
    return (outputs, input_grad, weight_grad)


def solution(mesh):
    finer = Mesh(mesh.devices.reshape(SPLIT), ("y", "zh", "x", "zl", "co"))
    specs = (P(CHAN, VOX, None), P(CHAN, VOX, None), P(CHAN, None, None))

    return jax.shard_map(local, mesh=finer, in_specs=specs, out_specs=specs, check_vma=False)


SPLIT = (4, 2, 4, 8, 2)
```
